32 devices in a mesh: grp: 4 (over z), dev: 8 (over y, x, core).
Axes of the slice: x: 2, y: 2, z: 4, core: 2. Of those that a mesh axis runs over, the one named last changes fastest.
Arguments:
- layer_inputs: bfloat16 [4, 4096, 4096], P(None, 'grp', 'dev')
- output_grads: bfloat16 [4, 4096, 2048], P(None, ('grp', 'dev'))
- layer_owner: int32 [4], replicated, may hold values from 0 to 3, each once
- master_weights: float32 [4, 4096, 2048], P('grp', 'dev')
- momentum: float32 [4, 4096, 2048], P('grp', 'dev'), may hold values from -6 to 6
- table_blocks: float32 [4, 64, 128, 128], P('grp', 'dev'), may hold values from -6 to 6
- block_grads: bfloat16 [4, 8, 16, 128, 128], P('grp', 'dev'), may hold values from -6 to 6
- block_ids: int32 [4, 8, 16], P('grp', 'dev'), may hold values from 0 to 7
- block_counts: int32 [4, 8, 8], P('grp', 'dev'), may hold values from 0 to 2, as said below
Outputs:
- new_master: float32 [4, 4096, 2048], P('grp', 'dev')
- new_momentum: float32 [4, 4096, 2048], P('grp', 'dev')
- new_weights: bfloat16 [4, 4096, 2048], P(None, 'dev')
- new_table: float32 [4, 64, 128, 128], P('grp', 'dev')
The draws below stay inside these ranges and needn't reach their ends.
Inputs may be any that keep to these rules, and one draw needn't show every extreme that they name: `layer_owner`: each group owns exactly one layer. `block_ids`: several live slots may name the same block; their gradients add. `block_counts`: in every group some owners receive 2 live slots from every device; slots at or past the count hold stale data.
All inputs are finite; a program needn't handle non-finite values.
Results may differ from the reference program's by a relative error of at most 0.001.
Values may be sent and summed in bfloat16 or wider, within the bound.
No kernel may reach another device: no remote copies, remote signals or barrier semaphores. Data moves between devices by JAX's collectives and lax.ppermute only.
A program may use at most 128 MiB of HBM per device.

```python
import jax
import jax.numpy as jnp
from jax import lax

D = 4096
OUTW = 2048
E = 128
BLK = 128
NB = 8
CAP = 2
LAYERS = 4
TOKENS = 4096
N_GRP = 4
N_DEV = 8


def feature_scale(key, count):
    spread = jax.random.uniform(key, (count,), jnp.float32)
    ramp = jnp.arange(count, dtype=jnp.float32) / count
    return 10.0 ** (spread - 0.5) * 3.0 ** (ramp - 0.5)


def column_scale(key, count):
    spread = jax.random.uniform(key, (count,), jnp.float32)
    return 10.0 ** (0.5 * (spread - 0.5))


def base_values(key, shape):
    first = jax.random.fold_in(key, 0)
    values = jax.random.normal(first, shape, jnp.float32)
    return values


def draw_layer_inputs(key, part):
    first, second = jax.random.split(jax.random.fold_in(key, 11))
    scale = feature_scale(first, D)
    values = base_values(second, (LAYERS, TOKENS, D))
    return (values * scale[None, None, :]).astype(jnp.bfloat16)


def draw_output_grads(key, part):
    first, second = jax.random.split(jax.random.fold_in(key, 23))
    scale = 0.02 * column_scale(first, OUTW)
    values = base_values(second, (LAYERS, TOKENS, OUTW))
    return (values * scale[None, None, :]).astype(jnp.bfloat16)


def draw_master_weights(key, part):
    first, second, third = jax.random.split(jax.random.fold_in(key, 37), 3)
    rows = feature_scale(first, D)
    cols = column_scale(second, OUTW)
    values = jax.random.normal(third, (N_GRP, D, OUTW), jnp.float32)
    return values * rows[None, :, None] * cols[None, None, :]


def draw_block_counts(key, part):
    first, second = jax.random.split(jax.random.fold_in(key, 53))
    hot_count = max(1, N_DEV // 8)
    offset = jax.random.randint(first, (N_GRP, 1), 0, N_DEV)
    hot = (jnp.arange(N_DEV, dtype=jnp.int32)[None, :] - offset) % N_DEV < hot_count
    other = jax.random.randint(second, (N_GRP, N_DEV, N_DEV), 0, CAP // 2 + 1)
    return jnp.where(hot[:, None, :], CAP, other).astype(jnp.int32)


def with_ends(values, key, low, largest):
    place = [jax.random.randint(jax.random.fold_in(key, axis), (), 0, length) for axis, length in enumerate(values.shape)]
    main_axis = values.shape.index(max(values.shape))
    beside = place[:main_axis] + [(place[main_axis] + 1) % values.shape[main_axis]] + place[main_axis + 1:]
    return values.at[tuple(place)].set(low).at[tuple(beside)].set(largest)


def shard_levels(key, shape, shards, least, high):
    level, own = 1.0, jax.random.fold_in(key, 6)
    for position, blocks in shards:
        heights = jnp.exp(jax.random.uniform(jax.random.fold_in(own, position), (blocks,), jnp.float32, least / len(shards), high / len(shards)))
        level = level * jnp.repeat(heights, shape[position] // blocks).reshape([-1 if axis == position else 1 for axis in range(len(shape))])
    return level


def gaussian(stream_key, extent, scale, limit, pieces=(), kind=jnp.bfloat16):
    values = scale * jax.random.normal(stream_key, extent, jnp.float32)
    if pieces:
        values = values * shard_levels(stream_key, extent, pieces, -0.22, 0.18)
    return jnp.clip(values, -limit, limit).astype(kind)


def setup_inputs(seed: int = 0) -> dict:
    seeds = jax.random.split(jax.random.key(seed), 10)
    layer_inputs = draw_layer_inputs(jax.random.fold_in(seeds[9], 71), 0)
    output_grads = draw_output_grads(jax.random.fold_in(seeds[9], 71), 0)
    layer_owner = jax.random.permutation(seeds[2], LAYERS).astype(jnp.int32)
    master_weights = draw_master_weights(jax.random.fold_in(seeds[9], 71), 0)
    momentum = gaussian(seeds[4], (N_GRP, D, OUTW), 1.0, 6.0, ((0, 4), (1, 8)), jnp.float32)
    table_blocks = gaussian(seeds[5], (N_GRP, N_DEV * NB, BLK, E), 1.0, 6.0, ((0, 4), (1, 8)), jnp.float32)
    block_grads = gaussian(seeds[6], (N_GRP, N_DEV, N_DEV * CAP, BLK, E), 1.0, 6.0, ((0, 4), (1, 8)))
    block_ids = with_ends(jax.random.randint(seeds[7], (N_GRP, N_DEV, N_DEV * CAP), 0, NB), jax.random.fold_in(seeds[7], 1), 0, NB - 1).astype(jnp.int32)
    block_counts = draw_block_counts(jax.random.fold_in(seeds[9], 71), 0)
    return {"layer_inputs": layer_inputs, "output_grads": output_grads, "layer_owner": layer_owner, "master_weights": master_weights, "momentum": momentum, "table_blocks": table_blocks, "block_grads": block_grads, "block_ids": block_ids, "block_counts": block_counts}


tower_rate = 0.5
momentum_keep = 0.9
tower_decay = 0.1
table_rate = 0.5
table_decay = 0.2
eps_norm = 1e-06

def reference(layer_inputs, output_grads, layer_owner, master_weights, momentum, table_blocks, block_grads, block_ids, block_counts):
    slot_layer = jnp.argsort(layer_owner).astype(jnp.int32)

    def layer_grad(index):
        inputs = layer_inputs[index].astype(jnp.float32)
        cotangent = output_grads[index].astype(jnp.float32)
        return jnp.dot(inputs.T, cotangent, precision=lax.Precision.HIGHEST)
    grad = lax.map(layer_grad, slot_layer)
    weight_sq = lax.optimization_barrier(jnp.sum(master_weights * master_weights, axis=(1, 2)))
    grad_sq = lax.optimization_barrier(jnp.sum(grad * grad, axis=(1, 2)))
    weight_norm = jnp.sqrt(weight_sq + eps_norm)
    trust = weight_norm / (jnp.sqrt(grad_sq + eps_norm) + tower_decay * weight_norm)
    new_momentum = momentum_keep * momentum + tower_rate * trust[:, None, None] * (grad + tower_decay * master_weights)
    new_master = master_weights - new_momentum
    new_weights = new_master[layer_owner.astype(jnp.int32)].astype(jnp.bfloat16)
    ndev = block_counts.shape[1]
    cap = block_ids.shape[2] // ndev
    nblocks = table_blocks.shape[1]
    width = table_blocks.shape[2] * table_blocks.shape[3]
    slot_index = jnp.arange(ndev * cap, dtype=jnp.int32)
    owner_of_slot = slot_index // cap

    def group_update(items):
        grads_g, ids_g, counts_g, table_g = items
        live = (slot_index % cap)[None, :] < jnp.repeat(counts_g, cap, axis=1)
        target = owner_of_slot[None, :] * (nblocks // ndev) + ids_g
        target = jnp.where(live, target, nblocks).reshape(-1)
        data = grads_g.reshape(ndev * ndev * cap, width).astype(jnp.float32)
        sums = jax.ops.segment_sum(data, target, num_segments=nblocks + 1)[:nblocks]
        hits = jax.ops.segment_sum(live.reshape(-1).astype(jnp.int32), target, num_segments=nblocks + 1)[:nblocks]
        flat = table_g.reshape(nblocks, width)
        w_norm = jnp.sqrt(lax.optimization_barrier(jnp.sum(flat * flat, axis=1)) + eps_norm)
        g_norm = jnp.sqrt(lax.optimization_barrier(jnp.sum(sums * sums, axis=1)) + eps_norm)
        block_trust = w_norm / (g_norm + table_decay * w_norm)
        moved = flat - table_rate * block_trust[:, None] * (sums + table_decay * flat)
        return jnp.where((hits > 0)[:, None], moved, flat).reshape(table_g.shape)
    new_table = lax.map(group_update, (block_grads, block_ids, block_counts, table_blocks))
    return (new_master, new_momentum, new_weights, new_table)
```

```python
import jax
import jax.numpy as jnp
from jax import lax
from jax.sharding import PartitionSpec as P

tower_rate = 0.5
momentum_keep = 0.9
tower_decay = 0.1
table_rate = 0.5
table_decay = 0.2
eps_norm = 1e-06
weight_chunks = 4


def after(value, *others):
    return lax.optimization_barrier((value, *others))[0]


def local(
    layer_inputs,
    output_grads,
    layer_owner,
    master_weights,
    momentum,
    table_blocks,
    block_grads,
    block_ids,
    block_counts,
):
    groups = lax.axis_size("grp")
    devices = lax.axis_size("dev")
    group = lax.axis_index("grp")
    device = lax.axis_index("dev")
    even = [mask for mask in range(devices) if mask % 2 == 0]
    order = jnp.array(even + [mask + 1 for mask in even], dtype=jnp.int32)

    def swap(value, mask):
        return lax.ppermute(value, "dev", [(i, i ^ mask) for i in range(devices)])

    def shift(value, step):
        return lax.ppermute(value, "grp", [(i, (i + step) % groups) for i in range(groups)])

    def dev_sum(value):
        pair = value + swap(value, 1)
        return pair + sum(swap(pair, mask) for mask in even[1:])

    def dev_gather(piece):
        near = jnp.concatenate([piece] + [swap(piece, mask) for mask in even[1:]], axis=0)
        return jnp.concatenate([near, swap(near, 1)], axis=0)

    layers = jnp.arange(groups, dtype=jnp.int32)
    slot_layer = jnp.sum(
        jnp.where(layer_owner[None, :] == layers[:, None], layers[None, :], 0), axis=1
    )
    master = master_weights[0]
    moment = momentum[0]
    rows, columns = master.shape
    tokens = layer_inputs.shape[1]
    per_dev = output_grads.shape[1]

    steps = [0]
    for step in range(1, groups // 2 + 1):
        steps += [step] if 2 * step == groups else [step, groups - step]
    g_own, x_own = {}, {}
    blocks = order ^ device
    for step in steps:
        layer = slot_layer[(group + step) % groups]
        g_send = lax.dynamic_index_in_dim(output_grads, layer, 0, keepdims=False)
        g_own[step] = shift(g_send, step) if step else g_send
    for step in steps:
        layer = slot_layer[(group + step) % groups]
        x_send = lax.dynamic_index_in_dim(layer_inputs, layer, 0, keepdims=False)
        x_send = x_send.reshape(devices, per_dev, rows)
        x_send = jnp.concatenate(
            [lax.dynamic_index_in_dim(x_send, blocks[i], 0) for i in range(devices)], axis=0
        ).reshape(tokens, rows)
        if step:
            x_send = shift(after(x_send, g_own[step]), step)
        x_own[step] = x_send

    weight_norm = jnp.sqrt(dev_sum(jnp.sum(master * master)) + eps_norm)

    grad = None
    for step in steps:
        part = lax.dot_general(
            x_own[step],
            dev_gather(g_own[step]),
            (((0,), (0,)), ((), ())),
            preferred_element_type=jnp.float32,
        )
        grad = part if grad is None else grad + part
    grad_norm = jnp.sqrt(dev_sum(jnp.sum(grad * grad)) + eps_norm)
    trust = weight_norm / (grad_norm + tower_decay * weight_norm)

    def update(grad, moment, master):
        new_moment = momentum_keep * moment + tower_rate * trust * (grad + tower_decay * master)
        return new_moment, master - new_moment

    new_moment, new_master = update(grad, moment, master)

    height = rows // weight_chunks
    up = [(i, i + 1) for i in range(groups - 1)]
    down = [(i + 1, i) for i in range(groups - 1)]
    pieces, own = [], []
    for chunk in range(weight_chunks):
        cut = lambda value: lax.slice_in_dim(value, chunk * height, (chunk + 1) * height)
        piece = update(cut(grad), cut(moment), cut(master))[1].astype(jnp.bfloat16)
        own.append(piece)
        pieces.append([(piece, piece)])
    for step in range(1, groups):
        for chunk in range(weight_chunks):
            above, below = pieces[chunk][-1]
            pieces[chunk].append((lax.ppermute(above, "grp", up), lax.ppermute(below, "grp", down)))
    new_weights = jnp.zeros((groups, rows, columns), jnp.bfloat16)
    for step in range(groups):
        layer = slot_layer[(group - step) % groups]
        for chunk in range(weight_chunks):
            if step == 0:
                piece = own[chunk]
            else:
                piece = jnp.where(group >= step, pieces[chunk][step][0], pieces[chunk][groups - step][1])
            new_weights = lax.dynamic_update_slice(
                new_weights, piece[None], (layer, chunk * height, 0)
            )

    grads = block_grads[0, 0]
    ids = block_ids[0, 0]
    counts = block_counts[0, 0]
    capacity = ids.shape[0] // devices
    slot_rank = jnp.arange(devices * capacity, dtype=jnp.int32) % capacity
    live = slot_rank < jnp.repeat(counts, capacity)
    tagged = jnp.where(live, ids, -1)
    got_grads, got_ids = (
        lax.all_to_all(grads, "dev", split_axis=0, concat_axis=0, tiled=True),
        lax.all_to_all(tagged, "dev", split_axis=0, concat_axis=0, tiled=True),
    )
    table = table_blocks[0]
    nblocks = table.shape[0]
    width = table.shape[1] * table.shape[2]
    matches = got_ids[None, :] == jnp.arange(nblocks, dtype=jnp.int32)[:, None]
    block_sum = jnp.dot(
        matches.astype(jnp.bfloat16),
        got_grads.reshape(got_ids.shape[0], width),
        preferred_element_type=jnp.float32,
    )
    hits = jnp.sum(matches.astype(jnp.int32), axis=1)
    flat = table.reshape(nblocks, width)
    w_norm = jnp.sqrt(jnp.sum(flat * flat, axis=1) + eps_norm)
    g_norm = jnp.sqrt(jnp.sum(block_sum * block_sum, axis=1) + eps_norm)
    block_trust = w_norm / (g_norm + table_decay * w_norm)
    moved = flat - table_rate * block_trust[:, None] * (block_sum + table_decay * flat)
    new_table = jnp.where((hits > 0)[:, None], moved, flat).reshape(table.shape)
    return (new_master[None], new_moment[None], new_weights, new_table[None])


def solution(mesh):
    return jax.shard_map(
        local,
        mesh=mesh,
        in_specs=(
            P(None, "grp", "dev"),
            P(None, ("grp", "dev"), None),
            P(),
            P("grp", "dev", None),
            P("grp", "dev", None),
            P("grp", "dev", None, None),
            P("grp", "dev", None, None, None),
            P("grp", "dev", None),
            P("grp", "dev", None),
        ),
        out_specs=(
            P("grp", "dev", None),
            P("grp", "dev", None),
            P(None, "dev", None),
            P("grp", "dev", None, None),
        ),
        check_vma=False,
    )
```

```python
import functools

import jax
import jax.numpy as jnp
from jax import lax
from jax.experimental import pallas as pl
from jax.experimental.pallas import tpu as pltpu
from jax.sharding import PartitionSpec as P

tower_rate = 0.5
momentum_keep = 0.9
tower_decay = 0.1
table_rate = 0.5
table_decay = 0.2
eps_norm = 1e-06
weight_chunks = 4
lanes = 128
vmem_bytes = 48 << 20


anywhere = pl.BlockSpec(memory_space=pl.ANY)


def accumulate(acc, inputs, near, far, last):
    devices = lax.axis_size("dev")
    half = devices // 2
    count = len(inputs)
    rows, tokens = inputs[0].shape
    per_dev = tokens // devices
    columns = near.shape[1]
    tile = min(columns, 512)
    tiles = columns // tile

    def kernel(*refs):
        refs = list(refs)
        acc_ref = refs.pop(0) if acc is not None else None
        x_refs = [refs.pop(0) for _ in range(count)]
        near_ref, far_ref, out_ref = refs.pop(0), refs.pop(0), refs.pop(0)
        square_ref = refs.pop(0) if last else None
        x_all, g_all, x_sem, g_sem = refs
        column = pl.program_id(0)
        device = lax.axis_index("dev")

        @pl.when(column == 0)
        def _():
            for i in range(count):
                pltpu.make_async_copy(x_refs[i], x_all.at[i], x_sem).start()
            for t in range(tiles):
                for side, ref in enumerate((near_ref, far_ref)):
                    for place in range(half):
                        owner = device ^ (2 * place + side)
                        for i in range(count):
                            pltpu.make_async_copy(
                                ref.at[
                                    pl.ds((place * count + i) * per_dev, per_dev),
                                    pl.ds(t * tile, tile),
                                ],
                                g_all.at[t, i, pl.ds(pl.multiple_of(owner * per_dev, per_dev), per_dev)],
                                g_sem.at[t],
                            ).start()
            pltpu.make_async_copy(x_all, x_all, x_sem).wait()

        pltpu.make_async_copy(g_all.at[column], g_all.at[column], g_sem.at[column]).wait()
        total = acc_ref[...] if acc is not None else None
        for i in range(count):
            part = jnp.dot(x_all[i], g_all[column, i], preferred_element_type=jnp.float32)
            total = part if total is None else total + part
        out_ref[...] = total
        if last:
            squares = jnp.sum(total * total, axis=0, keepdims=True)
            folded = sum(squares[:, k * lanes : (k + 1) * lanes] for k in range(tile // lanes))

            @pl.when(column == 0)
            def _():
                square_ref[...] = folded

            @pl.when(column > 0)
            def _():
                square_ref[...] += folded

    block = pl.BlockSpec((rows, tile), lambda j: (0, j))
    operands = ([acc] if acc is not None else []) + list(inputs) + [near, far]
    out_shape = [jax.ShapeDtypeStruct((rows, columns), jnp.float32)]
    out_specs = [block]
    if last:
        out_shape.append(jax.ShapeDtypeStruct((1, lanes), jnp.float32))
        out_specs.append(pl.BlockSpec((1, lanes), lambda j: (0, 0)))
    result = pl.pallas_call(
        kernel,
        grid=(tiles,),
        in_specs=([block] if acc is not None else []) + [anywhere] * (count + 2),
        out_specs=out_specs,
        out_shape=out_shape,
        scratch_shapes=[
            pltpu.VMEM((count, rows, tokens), jnp.bfloat16),
            pltpu.VMEM((tiles, count, tokens, tile), jnp.bfloat16),
            pltpu.SemaphoreType.DMA,
            pltpu.SemaphoreType.DMA((tiles,)),
        ],
        compiler_params=pltpu.CompilerParams(vmem_limit_bytes=vmem_bytes),
        cost_estimate=pl.CostEstimate(
            flops=2 * count * rows * tokens * columns,
            bytes_accessed=2 * count * tokens * (rows + columns) + 8 * rows * columns,
            transcendentals=0,
        ),
        name="accumulate",
    )(*operands)
    return result if last else result[0]


def update(slot_layer, weight_squares, grad_squares, grad, master, moment, chunk, buffers):
    groups = lax.axis_size("grp")
    rows, columns = grad.shape
    height = rows // weight_chunks
    step = min(height, 64)
    steps = height // step
    count = len(weight_squares)

    def kernel(slot_ref, *refs):
        refs = list(refs)
        weight_refs = [refs.pop(0) for _ in range(count)]
        grad_refs = [refs.pop(0) for _ in range(count)]
        grad_ref, master_ref, moment_ref = refs[:3]
        piece_ref, weights_out, master_out, moment_out = refs[-4:]

        def norm(parts):
            total = sum(ref[...] for ref in parts)
            return jnp.sqrt(jnp.sum(total, axis=1, keepdims=True) + eps_norm)

        weight_norm = norm(weight_refs)
        trust = weight_norm / (norm(grad_refs) + tower_decay * weight_norm)
        value = master_ref[...]
        new_moment = momentum_keep * moment_ref[...] + tower_rate * trust * (
            grad_ref[...] + tower_decay * value
        )
        new_master = value - new_moment
        moment_out[...] = new_moment
        master_out[...] = new_master
        piece = new_master.astype(jnp.bfloat16)
        piece_ref[...] = piece
        weights_out[0] = piece

    vector = pl.BlockSpec((1, lanes), lambda i, slot: (0, 0))
    block = pl.BlockSpec((step, columns), lambda i, slot: (chunk * steps + i, 0))
    operands = [slot_layer, *weight_squares, *grad_squares, grad, master, moment]
    first = len(operands)
    return pl.pallas_call(
        kernel,
        grid_spec=pltpu.PrefetchScalarGridSpec(
            num_scalar_prefetch=1,
            grid=(steps,),
            in_specs=[vector] * (2 * count) + [block] * 3 + [anywhere] * len(buffers),
            out_specs=[
                pl.BlockSpec((step, columns), lambda i, slot: (i, 0)),
                pl.BlockSpec(
                    (1, step, columns),
                    lambda i, slot: (slot[lax.axis_index("grp")], chunk * steps + i, 0),
                ),
                block,
                block,
            ],
        ),
        out_shape=[
            jax.ShapeDtypeStruct((height, columns), jnp.bfloat16),
            jax.ShapeDtypeStruct((groups, rows, columns), jnp.bfloat16),
            jax.ShapeDtypeStruct((rows, columns), jnp.float32),
            jax.ShapeDtypeStruct((rows, columns), jnp.float32),
        ],
        input_output_aliases={first + i: 1 + i for i in range(len(buffers))},
        cost_estimate=pl.CostEstimate(
            flops=8 * height * columns, bytes_accessed=24 * height * columns, transcendentals=0
        ),
        name="update",
    )(*operands, *buffers)


def place(slot_layer, weights, above, below, step, chunk):
    groups = lax.axis_size("grp")
    height, columns = above.shape

    def kernel(slot_ref, weights_ref, above_ref, below_ref, out_ref, held, in_sem, out_sem):
        group = lax.axis_index("grp")
        sides = (
            (above_ref, group - step, group >= step),
            (below_ref, group + step, group + step < groups),
        )
        for side, (ref, source, valid) in enumerate(sides):

            @pl.when(valid)
            def _():
                pltpu.make_async_copy(ref, held.at[side], in_sem.at[side]).start()

        for side, (ref, source, valid) in enumerate(sides):

            @pl.when(valid)
            def _():
                pltpu.make_async_copy(ref, held.at[side], in_sem.at[side]).wait()
                layer = slot_ref[source]
                copy = pltpu.make_async_copy(
                    held.at[side], out_ref.at[layer, pl.ds(chunk * height, height)], out_sem.at[side]
                )
                copy.start()

        for side, (ref, source, valid) in enumerate(sides):

            @pl.when(valid)
            def _():
                pltpu.make_async_copy(
                    held.at[side], out_ref.at[0, pl.ds(chunk * height, height)], out_sem.at[side]
                ).wait()

    return pl.pallas_call(
        kernel,
        grid_spec=pltpu.PrefetchScalarGridSpec(
            num_scalar_prefetch=1,
            grid=(1,),
            in_specs=[anywhere] * 3,
            out_specs=anywhere,
            scratch_shapes=[
                pltpu.VMEM((2, height, columns), jnp.bfloat16),
                pltpu.SemaphoreType.DMA((2,)),
                pltpu.SemaphoreType.DMA((2,)),
            ],
        ),
        out_shape=jax.ShapeDtypeStruct(weights.shape, weights.dtype),
        input_output_aliases={1: 0},
        cost_estimate=pl.CostEstimate(
            flops=0, bytes_accessed=8 * height * columns, transcendentals=0
        ),
        name="place",
    )(slot_layer, weights, above, below)


def local(
    layer_inputs,
    output_grads,
    layer_owner,
    master_weights,
    momentum,
    table_blocks,
    block_grads,
    block_ids,
    block_counts,
):
    groups = lax.axis_size("grp")
    devices = lax.axis_size("dev")
    group = lax.axis_index("grp")
    even = range(0, devices, 2)

    def swap(value, mask):
        return lax.ppermute(value, "dev", [(i, i ^ mask) for i in range(devices)])

    def shift(value, step):
        return lax.ppermute(value, "grp", [(i, (i + step) % groups) for i in range(groups)])

    def dev_parts(value):
        pair = value + swap(value, 1)
        return [pair] + [swap(pair, mask) for mask in even[1:]]

    def dev_gather(piece):
        near = jnp.concatenate([piece] + [swap(piece, mask) for mask in even[1:]], axis=0)
        return near, swap(near, 1)

    layers = jnp.arange(groups, dtype=jnp.int32)
    slot_layer = jnp.sum(
        jnp.where(layer_owner[None, :] == layers[:, None], layers[None, :], 0), axis=1
    )
    master = master_weights[0]
    moment = momentum[0]
    rows, columns = master.shape

    rounds = [[0]]
    for step in range(1, groups // 2 + 1):
        rounds.append([step] if 2 * step == groups else [step, groups - step])
    steps = [step for some in rounds for step in some]

    def owned(value, step):
        return lax.dynamic_index_in_dim(
            value, slot_layer[(group + step) % groups], 0, keepdims=False
        )

    g_own = {step: owned(output_grads, step) for step in steps}
    g_own = {step: shift(value, step) if step else value for step, value in g_own.items()}
    x_own = {step: owned(layer_inputs, step).T for step in steps}
    x_own = {step: shift(value, step) if step else value for step, value in x_own.items()}

    squares = jnp.sum(master * master, axis=0, keepdims=True)
    squares = jnp.sum(squares.reshape(columns // lanes, lanes), axis=0, keepdims=True)
    weight_squares = dev_parts(squares)

    grad = None
    for some in rounds:
        pieces = [g_own[step] for step in some]
        piece = jnp.concatenate(pieces, axis=0) if len(some) > 1 else pieces[0]
        near, far = dev_gather(piece)
        last = some is rounds[-1]
        grad = accumulate(grad, [x_own[step] for step in some], near, far, last)
    grad, squares = grad
    grad_squares = dev_parts(squares)

    up = [(i, i + 1) for i in range(groups - 1)]
    down = [(i + 1, i) for i in range(groups - 1)]
    buffers, above, below = [], [], []
    for chunk in range(weight_chunks):
        piece, *buffers = update(
            slot_layer, weight_squares, grad_squares, grad, master, moment, chunk, buffers
        )
        above.append(piece)
        below.append(piece)
    new_weights, new_master, new_moment = buffers
    for step in range(1, groups):
        for chunk in range(weight_chunks):
            above[chunk] = lax.ppermute(above[chunk], "grp", up)
            below[chunk] = lax.ppermute(below[chunk], "grp", down)
            new_weights = place(slot_layer, new_weights, above[chunk], below[chunk], step, chunk)

    grads = block_grads[0, 0]
    ids = block_ids[0, 0]
    counts = block_counts[0, 0]
    capacity = ids.shape[0] // devices
    slot_rank = jnp.arange(devices * capacity, dtype=jnp.int32) % capacity
    live = slot_rank < jnp.repeat(counts, capacity)
    tagged = jnp.where(live, ids, -1)
    got_grads, got_ids = (
        lax.all_to_all(grads, "dev", split_axis=0, concat_axis=0, tiled=True),
        lax.all_to_all(tagged, "dev", split_axis=0, concat_axis=0, tiled=True),
    )
    table = table_blocks[0]
    nblocks = table.shape[0]
    width = table.shape[1] * table.shape[2]
    matches = got_ids[None, :] == jnp.arange(nblocks, dtype=jnp.int32)[:, None]
    block_sum = jnp.dot(
        matches.astype(jnp.bfloat16),
        got_grads.reshape(got_ids.shape[0], width),
        preferred_element_type=jnp.float32,
    )
    hits = jnp.sum(matches.astype(jnp.int32), axis=1)
    flat = table.reshape(nblocks, width)
    w_norm = jnp.sqrt(jnp.sum(flat * flat, axis=1) + eps_norm)
    g_norm = jnp.sqrt(jnp.sum(block_sum * block_sum, axis=1) + eps_norm)
    block_trust = w_norm / (g_norm + table_decay * w_norm)
    moved = flat - table_rate * block_trust[:, None] * (block_sum + table_decay * flat)
    new_table = jnp.where((hits > 0)[:, None], moved, flat).reshape(table.shape)
    return (new_master[None], new_moment[None], new_weights, new_table[None])


def solution(mesh):
    return jax.shard_map(
        local,
        mesh=mesh,
        in_specs=(
            P(None, "grp", "dev"),
            P(None, ("grp", "dev"), None),
            P(),
            P("grp", "dev", None),
            P("grp", "dev", None),
            P("grp", "dev", None, None),
            P("grp", "dev", None, None, None),
            P("grp", "dev", None),
            P("grp", "dev", None),
        ),
        out_specs=(
            P("grp", "dev", None),
            P("grp", "dev", None),
            P(None, "dev", None),
            P("grp", "dev", None, None),
        ),
        check_vma=False,
    )
```

```python
import jax
import jax.numpy as jnp
from jax import lax
from jax.experimental import pallas as pl
from jax.experimental.pallas import tpu as pltpu
from jax.sharding import PartitionSpec as P


tower_rate = 0.5
momentum_keep = 0.9
tower_decay = 0.1
table_rate = 0.5
table_decay = 0.2
eps_norm = 1e-06
weight_chunks = 2
lanes = 128
mib = 1 << 20


anywhere = pl.BlockSpec(memory_space=pl.ANY)


def accumulate(acc, inputs, near, far, last):
    devices = lax.axis_size("dev")
    half = devices // 2
    count = len(inputs)
    rows, tokens = inputs[0].shape
    per_dev = tokens // devices
    columns = near.shape[1]
    tile = min(columns, 512)
    tiles = columns // tile

    def kernel(*refs):
        refs = list(refs)
        acc_ref = refs.pop(0) if acc is not None else None
        x_refs = [refs.pop(0) for _ in range(count)]
        near_ref, far_ref, out_ref = refs.pop(0), refs.pop(0), refs.pop(0)
        square_ref = refs.pop(0) if last else None
        x_all, g_all, x_sem, g_sem = refs
        column = pl.program_id(0)
        device = lax.axis_index("dev")

        @pl.when(column == 0)
        def _():
            for i in range(count):
                pltpu.make_async_copy(x_refs[i], x_all.at[i], x_sem).start()
            for t in range(tiles):
                for side, ref in enumerate((near_ref, far_ref)):
                    for place in range(half):
                        owner = device ^ (2 * place + side)
                        for i in range(count):
                            pltpu.make_async_copy(
                                ref.at[
                                    pl.ds((place * count + i) * per_dev, per_dev),
                                    pl.ds(t * tile, tile),
                                ],
                                g_all.at[t, i, pl.ds(pl.multiple_of(owner * per_dev, per_dev), per_dev)],
                                g_sem.at[t],
                            ).start()
            pltpu.make_async_copy(x_all, x_all, x_sem).wait()

        pltpu.make_async_copy(g_all.at[column], g_all.at[column], g_sem.at[column]).wait()
        total = acc_ref[...] if acc is not None else None
        for i in range(count):
            part = jnp.dot(x_all[i], g_all[column, i], preferred_element_type=jnp.float32)
            total = part if total is None else total + part
        out_ref[...] = total
        if last:
            squares = jnp.sum(total * total, axis=0, keepdims=True)
            folded = sum(squares[:, k * lanes : (k + 1) * lanes] for k in range(tile // lanes))

            @pl.when(column == 0)
            def _():
                square_ref[...] = folded

            @pl.when(column > 0)
            def _():
                square_ref[...] += folded

    block = pl.BlockSpec((rows, tile), lambda j: (0, j))
    operands = ([acc] if acc is not None else []) + list(inputs) + [near, far]
    out_shape = [jax.ShapeDtypeStruct((rows, columns), jnp.float32)]
    out_specs = [block]
    if last:
        out_shape.append(jax.ShapeDtypeStruct((1, lanes), jnp.float32))
        out_specs.append(pl.BlockSpec((1, lanes), lambda j: (0, 0)))
    result = pl.pallas_call(
        kernel,
        grid=(tiles,),
        in_specs=([block] if acc is not None else []) + [anywhere] * (count + 2),
        out_specs=out_specs,
        out_shape=out_shape,
        scratch_shapes=[
            pltpu.VMEM((count, rows, tokens), jnp.bfloat16),
            pltpu.VMEM((tiles, count, tokens, tile), jnp.bfloat16),
            pltpu.SemaphoreType.DMA,
            pltpu.SemaphoreType.DMA((tiles,)),
        ],
        compiler_params=pltpu.CompilerParams(
            vmem_limit_bytes=2 * count * tokens * (rows + columns) + 16 * rows * tile + 2 * mib
        ),
        cost_estimate=pl.CostEstimate(
            flops=2 * count * rows * tokens * columns,
            bytes_accessed=2 * count * tokens * (rows + columns) + 8 * rows * columns,
            transcendentals=0,
        ),
        name="accumulate",
    )(*operands)
    return result if last else result[0]


def update(slot_layer, weight_squares, grad_squares, grad, master, moment, chunk, buffers):
    groups = lax.axis_size("grp")
    rows, columns = grad.shape
    height = rows // weight_chunks
    step = min(height, 32)
    steps = height // step
    count = len(weight_squares)

    def kernel(slot_ref, *refs):
        refs = list(refs)
        weight_refs = [refs.pop(0) for _ in range(count)]
        grad_refs = [refs.pop(0) for _ in range(count)]
        grad_ref, master_ref, moment_ref = refs[:3]
        piece_ref, weights_out, master_out, moment_out = refs[-4:]

        def norm(parts):
            total = sum(ref[...] for ref in parts)
            return jnp.sqrt(jnp.sum(total, axis=1, keepdims=True) + eps_norm)

        weight_norm = norm(weight_refs)
        trust = weight_norm / (norm(grad_refs) + tower_decay * weight_norm)
        value = master_ref[...]
        new_moment = momentum_keep * moment_ref[...] + tower_rate * trust * (
            grad_ref[...] + tower_decay * value
        )
        new_master = value - new_moment
        moment_out[...] = new_moment
        master_out[...] = new_master
        piece = new_master.astype(jnp.bfloat16)
        piece_ref[...] = piece
        weights_out[0] = piece

    vector = pl.BlockSpec((1, lanes), lambda i, slot: (0, 0))
    block = pl.BlockSpec((step, columns), lambda i, slot: (chunk * steps + i, 0))
    operands = [slot_layer, *weight_squares, *grad_squares, grad, master, moment]
    first = len(operands)
    return pl.pallas_call(
        kernel,
        grid_spec=pltpu.PrefetchScalarGridSpec(
            num_scalar_prefetch=1,
            grid=(steps,),
            in_specs=[vector] * (2 * count) + [block] * 3 + [anywhere] * len(buffers),
            out_specs=[
                pl.BlockSpec((step, columns), lambda i, slot: (i, 0)),
                pl.BlockSpec(
                    (1, step, columns),
                    lambda i, slot: (slot[lax.axis_index("grp")], chunk * steps + i, 0),
                ),
                block,
                block,
            ],
        ),
        out_shape=[
            jax.ShapeDtypeStruct((height, columns), jnp.bfloat16),
            jax.ShapeDtypeStruct((groups, rows, columns), jnp.bfloat16),
            jax.ShapeDtypeStruct((rows, columns), jnp.float32),
            jax.ShapeDtypeStruct((rows, columns), jnp.float32),
        ],
        input_output_aliases={first + i: 1 + i for i in range(len(buffers))},
        compiler_params=pltpu.CompilerParams(vmem_limit_bytes=48 * step * columns + 2 * mib),
        cost_estimate=pl.CostEstimate(
            flops=8 * height * columns, bytes_accessed=24 * height * columns, transcendentals=0
        ),
        name="update",
    )(*operands, *buffers)


def place(slot_layer, weights, above, below, step, chunk):
    groups = lax.axis_size("grp")
    height, columns = above.shape

    def kernel(slot_ref, weights_ref, above_ref, below_ref, out_ref, held, in_sem, out_sem):
        group = lax.axis_index("grp")
        sides = (
            (above_ref, group - step, group >= step),
            (below_ref, group + step, group + step < groups),
        )
        for side, (ref, source, valid) in enumerate(sides):

            @pl.when(valid)
            def _():
                pltpu.make_async_copy(ref, held.at[side], in_sem.at[side]).start()

        for side, (ref, source, valid) in enumerate(sides):

            @pl.when(valid)
            def _():
                pltpu.make_async_copy(ref, held.at[side], in_sem.at[side]).wait()
                layer = slot_ref[source]
                copy = pltpu.make_async_copy(
                    held.at[side], out_ref.at[layer, pl.ds(chunk * height, height)], out_sem.at[side]
                )
                copy.start()

        for side, (ref, source, valid) in enumerate(sides):

            @pl.when(valid)
            def _():
                pltpu.make_async_copy(
                    held.at[side], out_ref.at[0, pl.ds(chunk * height, height)], out_sem.at[side]
                ).wait()

    return pl.pallas_call(
        kernel,
        grid_spec=pltpu.PrefetchScalarGridSpec(
            num_scalar_prefetch=1,
            grid=(1,),
            in_specs=[anywhere] * 3,
            out_specs=anywhere,
            scratch_shapes=[
                pltpu.VMEM((2, height, columns), jnp.bfloat16),
                pltpu.SemaphoreType.DMA((2,)),
                pltpu.SemaphoreType.DMA((2,)),
            ],
        ),
        out_shape=jax.ShapeDtypeStruct(weights.shape, weights.dtype),
        input_output_aliases={1: 0},
        compiler_params=pltpu.CompilerParams(vmem_limit_bytes=4 * height * columns + 2 * mib),
        cost_estimate=pl.CostEstimate(
            flops=0, bytes_accessed=8 * height * columns, transcendentals=0
        ),
        name="place",
    )(slot_layer, weights, above, below)


def rounds_of(groups):
    rounds = [[0]]
    for step in range(1, groups // 2 + 1):
        rounds.append([step] if 2 * step == groups else [step, groups - step])
    return rounds


def local(
    layer_inputs,
    output_grads,
    layer_owner,
    master_weights,
    momentum,
    table_blocks,
    block_grads,
    block_ids,
    block_counts,
):
    groups = lax.axis_size("grp")
    devices = lax.axis_size("dev")
    group = lax.axis_index("grp")
    masks = range(2, devices, 2)

    def swap(value, mask):
        return lax.ppermute(value, "dev", [(i, i ^ mask) for i in range(devices)])

    def shift(value, step):
        if step == 0:
            return value
        return lax.ppermute(value, "grp", [(i, (i + step) % groups) for i in range(groups)])

    def dev_parts(value):
        pair = value + swap(value, 1)
        return [pair] + [swap(pair, mask) for mask in masks]

    layers = jnp.arange(groups, dtype=jnp.int32)
    slot_layer = jnp.sum(
        jnp.where(layer_owner[None, :] == layers[:, None], layers[None, :], 0), axis=1
    )
    master = master_weights[0]
    moment = momentum[0]
    _, columns = master.shape

    rounds = rounds_of(groups)
    steps = [step for some in rounds for step in some]

    def owned(value, step):
        return lax.dynamic_index_in_dim(
            value, slot_layer[(group + step) % groups], 0, keepdims=False
        )

    g_own = {step: shift(owned(output_grads, step), step) for step in steps}
    x_own = {step: shift(owned(layer_inputs, step).T, step) for step in steps}

    squares = jnp.sum(master * master, axis=0, keepdims=True)
    squares = jnp.sum(squares.reshape(columns // lanes, lanes), axis=0, keepdims=True)
    weight_squares = dev_parts(squares)

    new_table = update_table(table_blocks[0], block_grads, block_ids, block_counts, g_own[steps[1]])

    grad = None
    for some in rounds:
        pieces = [g_own[step] for step in some]
        piece = jnp.concatenate(pieces, axis=0) if len(some) > 1 else pieces[0]
        near = jnp.concatenate([piece] + [swap(piece, mask) for mask in masks], axis=0)
        far = swap(near, 1)
        inputs = [x_own[step] for step in some]
        last = some is rounds[-1]
        if last:
            inputs[0], new_table = lax.optimization_barrier((inputs[0], new_table))
        grad = accumulate(grad, inputs, near, far, last)
    grad, squares = grad
    grad_squares = dev_parts(squares)

    up = [(i, i + 1) for i in range(groups - 1)]
    down = [(i + 1, i) for i in range(groups - 1)]
    buffers, above, below = [], [], []
    for chunk in range(weight_chunks):
        piece, *buffers = update(
            slot_layer, weight_squares, grad_squares, grad, master, moment, chunk, buffers
        )
        above.append(piece)
        below.append(piece)
    new_weights, new_master, new_moment = buffers
    for step in range(1, groups):
        for chunk in range(weight_chunks):
            above[chunk] = lax.ppermute(above[chunk], "grp", up)
            below[chunk] = lax.ppermute(below[chunk], "grp", down)
            new_weights = place(slot_layer, new_weights, above[chunk], below[chunk], step, chunk)
    return (new_master[None], new_moment[None], new_weights, new_table[None])


def update_table(table, block_grads, block_ids, block_counts, behind):
    devices = lax.axis_size("dev")
    grads, ids, _ = lax.optimization_barrier((block_grads[0, 0], block_ids[0, 0], behind))
    counts = block_counts[0, 0]
    capacity = ids.shape[0] // devices
    slot_rank = jnp.arange(devices * capacity, dtype=jnp.int32) % capacity
    live = slot_rank < jnp.repeat(counts, capacity)
    tagged = jnp.where(live, ids, -1)
    got_grads, got_ids = (
        lax.all_to_all(grads, "dev", split_axis=0, concat_axis=0, tiled=True),
        lax.all_to_all(tagged, "dev", split_axis=0, concat_axis=0, tiled=True),
    )
    nblocks = table.shape[0]
    width = table.shape[1] * table.shape[2]
    matches = got_ids[None, :] == jnp.arange(nblocks, dtype=jnp.int32)[:, None]
    block_sum = jnp.dot(
        matches.astype(jnp.bfloat16),
        got_grads.reshape(got_ids.shape[0], width),
        preferred_element_type=jnp.float32,
    )
    hits = jnp.sum(matches.astype(jnp.int32), axis=1)
    flat = table.reshape(nblocks, width)
    w_norm = jnp.sqrt(jnp.sum(flat * flat, axis=1) + eps_norm)
    g_norm = jnp.sqrt(jnp.sum(block_sum * block_sum, axis=1) + eps_norm)
    block_trust = w_norm / (g_norm + table_decay * w_norm)
    moved = flat - table_rate * block_trust[:, None] * (block_sum + table_decay * flat)
    return jnp.where((hits > 0)[:, None], moved, flat).reshape(table.shape)


def solution(mesh):
    return jax.shard_map(
        local,
        mesh=mesh,
        in_specs=(
            P(None, "grp", "dev"),
            P(None, ("grp", "dev"), None),
            P(),
            P("grp", "dev", None),
            P("grp", "dev", None),
            P("grp", "dev", None, None),
            P("grp", "dev", None, None, None),
            P("grp", "dev", None),
            P("grp", "dev", None),
        ),
        out_specs=(
            P("grp", "dev", None),
            P("grp", "dev", None),
            P(None, "dev", None),
            P("grp", "dev", None, None),
        ),
        check_vma=False,
    )
```

```python
import jax
import jax.numpy as jnp
from jax import lax
from jax.experimental import pallas as pl
from jax.experimental.pallas import tpu as pltpu
from jax.sharding import PartitionSpec as P


tower_rate = 0.5
momentum_keep = 0.9
tower_decay = 0.1
table_rate = 0.5
table_decay = 0.2
eps_norm = 1e-06
weight_parts = (1, 6, 1)
lanes = 128
mib = 1 << 20


anywhere = pl.BlockSpec(memory_space=pl.ANY)


def layer_of(owner_ref, target):
    return sum(jnp.where(owner_ref[layer] == target, layer, 0) for layer in range(owner_ref.shape[0]))


def chunks_of(rows):
    unit = rows // sum(weight_parts)
    starts = [unit * sum(weight_parts[:i]) for i in range(len(weight_parts))]
    return [(start, unit * part) for start, part in zip(starts, weight_parts)]


def pick(layer_owner, value, steps):
    groups = lax.axis_size("grp")
    count = len(steps)

    def kernel(owner_ref, value_ref, *refs):
        sems = refs[count]
        group = lax.axis_index("grp")
        copies = [
            pltpu.make_async_copy(
                value_ref.at[layer_of(owner_ref, lax.rem(group + step, groups))],
                refs[i],
                sems.at[i],
            )
            for i, step in enumerate(steps)
        ]
        for copy in copies:
            copy.start()
        for copy in copies:
            copy.wait()

    shape = value.shape[1:]
    return pl.pallas_call(
        kernel,
        grid_spec=pltpu.PrefetchScalarGridSpec(
            num_scalar_prefetch=1,
            grid=(1,),
            in_specs=[anywhere],
            out_specs=[pl.BlockSpec(shape, lambda i, owner: (0, 0))] * count,
            scratch_shapes=[pltpu.SemaphoreType.DMA((count,))],
        ),
        out_shape=[jax.ShapeDtypeStruct(shape, value.dtype)] * count,
        compiler_params=pltpu.CompilerParams(
            vmem_limit_bytes=4 * count * shape[0] * shape[1] + 2 * mib
        ),
        cost_estimate=pl.CostEstimate(
            flops=0, bytes_accessed=4 * count * shape[0] * shape[1], transcendentals=0
        ),
        name="pick",
    )(layer_owner, value)


def accumulate(acc, inputs, near, far, last):
    devices = lax.axis_size("dev")
    half = devices // 2
    count = len(inputs)
    rows, tokens = inputs[0].shape
    per_dev = tokens // devices
    columns = near.shape[1]
    tile = min(columns, 512)
    tiles = columns // tile

    def kernel(*refs):
        refs = list(refs)
        acc_ref = refs.pop(0) if acc is not None else None
        x_refs = [refs.pop(0) for _ in range(count)]
        near_ref, far_ref, out_ref = refs.pop(0), refs.pop(0), refs.pop(0)
        square_ref = refs.pop(0) if last else None
        x_all, g_all, x_sem, g_sem = refs
        column = pl.program_id(0)
        device = lax.axis_index("dev")

        @pl.when(column == 0)
        def _():
            for i in range(count):
                pltpu.make_async_copy(x_refs[i], x_all.at[i], x_sem).start()
            for t in range(tiles):
                for side, ref in enumerate((near_ref, far_ref)):
                    for place in range(half):
                        owner = device ^ (2 * place + side)
                        for i in range(count):
                            pltpu.make_async_copy(
                                ref.at[
                                    pl.ds((place * count + i) * per_dev, per_dev),
                                    pl.ds(t * tile, tile),
                                ],
                                g_all.at[t, i, pl.ds(pl.multiple_of(owner * per_dev, per_dev), per_dev)],
                                g_sem.at[t],
                            ).start()
            pltpu.make_async_copy(x_all, x_all, x_sem).wait()

        pltpu.make_async_copy(g_all.at[column], g_all.at[column], g_sem.at[column]).wait()
        total = acc_ref[...] if acc is not None else None
        for i in range(count):
            part = jnp.dot(x_all[i], g_all[column, i], preferred_element_type=jnp.float32)
            total = part if total is None else total + part
        out_ref[...] = total
        if last:
            squares = jnp.sum(total * total, axis=0, keepdims=True)
            folded = sum(squares[:, k * lanes : (k + 1) * lanes] for k in range(tile // lanes))

            @pl.when(column == 0)
            def _():
                square_ref[...] = folded

            @pl.when(column > 0)
            def _():
                square_ref[...] += folded

    block = pl.BlockSpec((rows, tile), lambda j: (0, j))
    operands = ([acc] if acc is not None else []) + list(inputs) + [near, far]
    out_shape = [jax.ShapeDtypeStruct((rows, columns), jnp.float32)]
    out_specs = [block]
    if last:
        out_shape.append(jax.ShapeDtypeStruct((1, lanes), jnp.float32))
        out_specs.append(pl.BlockSpec((1, lanes), lambda j: (0, 0)))
    result = pl.pallas_call(
        kernel,
        grid=(tiles,),
        in_specs=([block] if acc is not None else []) + [anywhere] * (count + 2),
        out_specs=out_specs,
        out_shape=out_shape,
        scratch_shapes=[
            pltpu.VMEM((count, rows, tokens), jnp.bfloat16),
            pltpu.VMEM((tiles, count, tokens, tile), jnp.bfloat16),
            pltpu.SemaphoreType.DMA,
            pltpu.SemaphoreType.DMA((tiles,)),
        ],
        compiler_params=pltpu.CompilerParams(
            vmem_limit_bytes=2 * count * tokens * (rows + columns) + 16 * rows * tile + 2 * mib
        ),
        cost_estimate=pl.CostEstimate(
            flops=2 * count * rows * tokens * columns,
            bytes_accessed=2 * count * tokens * (rows + columns) + 8 * rows * columns,
            transcendentals=0,
        ),
        name="accumulate",
    )(*operands)
    return result if last else result[0]


def update(layer_owner, weight_squares, grad_squares, grad, master, moment, chunk, buffers):
    groups = lax.axis_size("grp")
    rows, columns = grad.shape
    start, height = chunk
    step = min(32, rows // sum(weight_parts))
    first, steps = start // step, height // step
    count = len(weight_squares)

    def kernel(owner_ref, *refs):
        refs = list(refs)
        weight_refs = [refs.pop(0) for _ in range(count)]
        grad_refs = [refs.pop(0) for _ in range(count)]
        grad_ref, master_ref, moment_ref = refs[:3]
        piece_ref, weights_out, master_out, moment_out = refs[-4:]

        def norm(parts):
            total = sum(ref[...] for ref in parts)
            return jnp.sqrt(jnp.sum(total, axis=1, keepdims=True) + eps_norm)

        weight_norm = norm(weight_refs)
        trust = weight_norm / (norm(grad_refs) + tower_decay * weight_norm)
        value = master_ref[...]
        new_moment = momentum_keep * moment_ref[...] + tower_rate * trust * (
            grad_ref[...] + tower_decay * value
        )
        new_master = value - new_moment
        moment_out[...] = new_moment
        master_out[...] = new_master
        piece = new_master.astype(jnp.bfloat16)
        piece_ref[...] = piece
        weights_out[0] = piece

    vector = pl.BlockSpec((1, lanes), lambda i, owner: (0, 0))
    block = pl.BlockSpec((step, columns), lambda i, owner: (first + i, 0))
    operands = [layer_owner, *weight_squares, *grad_squares, grad, master, moment]
    taken = len(operands)
    return pl.pallas_call(
        kernel,
        grid_spec=pltpu.PrefetchScalarGridSpec(
            num_scalar_prefetch=1,
            grid=(steps,),
            in_specs=[vector] * (2 * count) + [block] * 3 + [anywhere] * len(buffers),
            out_specs=[
                pl.BlockSpec((step, columns), lambda i, owner: (i, 0)),
                pl.BlockSpec(
                    (1, step, columns),
                    lambda i, owner: (layer_of(owner, lax.axis_index("grp")), first + i, 0),
                ),
                block,
                block,
            ],
        ),
        out_shape=[
            jax.ShapeDtypeStruct((height, columns), jnp.bfloat16),
            jax.ShapeDtypeStruct((groups, rows, columns), jnp.bfloat16),
            jax.ShapeDtypeStruct((rows, columns), jnp.float32),
            jax.ShapeDtypeStruct((rows, columns), jnp.float32),
        ],
        input_output_aliases={taken + i: 1 + i for i in range(len(buffers))},
        compiler_params=pltpu.CompilerParams(vmem_limit_bytes=48 * step * columns + 2 * mib),
        cost_estimate=pl.CostEstimate(
            flops=8 * height * columns, bytes_accessed=24 * height * columns, transcendentals=0
        ),
        name="update",
    )(*operands, *buffers)


def place(layer_owner, weights, above, below, step, chunk):
    groups = lax.axis_size("grp")
    columns = above.shape[1]
    start, height = chunk

    def kernel(owner_ref, weights_ref, above_ref, below_ref, out_ref, held, in_sem, out_sem):
        group = lax.axis_index("grp")
        sides = (
            (above_ref, group - step, group >= step),
            (below_ref, group + step, group + step < groups),
        )
        for side, (ref, source, valid) in enumerate(sides):

            @pl.when(valid)
            def _():
                pltpu.make_async_copy(ref, held.at[side], in_sem.at[side]).start()

        for side, (ref, source, valid) in enumerate(sides):

            @pl.when(valid)
            def _():
                pltpu.make_async_copy(ref, held.at[side], in_sem.at[side]).wait()
                layer = layer_of(owner_ref, source)
                copy = pltpu.make_async_copy(
                    held.at[side], out_ref.at[layer, pl.ds(start, height)], out_sem.at[side]
                )
                copy.start()

        for side, (ref, source, valid) in enumerate(sides):

            @pl.when(valid)
            def _():
                pltpu.make_async_copy(
                    held.at[side], out_ref.at[0, pl.ds(start, height)], out_sem.at[side]
                ).wait()

    return pl.pallas_call(
        kernel,
        grid_spec=pltpu.PrefetchScalarGridSpec(
            num_scalar_prefetch=1,
            grid=(1,),
            in_specs=[anywhere] * 3,
            out_specs=anywhere,
            scratch_shapes=[
                pltpu.VMEM((2, height, columns), jnp.bfloat16),
                pltpu.SemaphoreType.DMA((2,)),
                pltpu.SemaphoreType.DMA((2,)),
            ],
        ),
        out_shape=jax.ShapeDtypeStruct(weights.shape, weights.dtype),
        input_output_aliases={1: 0},
        compiler_params=pltpu.CompilerParams(vmem_limit_bytes=4 * height * columns + 2 * mib),
        cost_estimate=pl.CostEstimate(
            flops=0, bytes_accessed=8 * height * columns, transcendentals=0
        ),
        name="place",
    )(layer_owner, weights, above, below)


def rounds_of(groups):
    rounds = [[0]]
    for step in range(1, groups // 2 + 1):
        rounds.append([step] if 2 * step == groups else [step, groups - step])
    return rounds


def local(
    layer_inputs,
    output_grads,
    layer_owner,
    master_weights,
    momentum,
    table_blocks,
    block_grads,
    block_ids,
    block_counts,
):
    groups = lax.axis_size("grp")
    devices = lax.axis_size("dev")
    group = lax.axis_index("grp")
    masks = range(2, devices, 2)

    def swap(value, mask):
        return lax.ppermute(value, "dev", [(i, i ^ mask) for i in range(devices)])

    def shift(value, step):
        if step == 0:
            return value
        return lax.ppermute(value, "grp", [(i, (i + step) % groups) for i in range(groups)])

    def dev_parts(value):
        pair = value + swap(value, 1)
        return [pair] + [swap(pair, mask) for mask in masks]

    master = master_weights[0]
    moment = momentum[0]
    rows, columns = master.shape

    rounds = rounds_of(groups)
    steps = [step for some in rounds for step in some]

    layers = jnp.arange(groups, dtype=jnp.int32)

    def owned(value, step):
        target = (group + step) % groups
        layer = jnp.sum(jnp.where(layer_owner == target, layers, 0)).astype(jnp.uint32)
        return lax.dynamic_index_in_dim(value, layer, 0, keepdims=False)

    g_own = dict(zip(steps, pick(layer_owner, output_grads, steps)))
    new_table = update_table(table_blocks[0], block_grads[0, 0], block_ids[0, 0], block_counts[0, 0])
    g_own = {step: shift(g_own[step], step) for step in steps}
    x_own = {step: shift(owned(layer_inputs, step).T, step) for step in steps}

    squares = jnp.sum(master * master, axis=0, keepdims=True)
    squares = jnp.sum(squares.reshape(columns // lanes, lanes), axis=0, keepdims=True)
    weight_squares = dev_parts(squares)

    grad = None
    for some in rounds:
        pieces = [g_own[step] for step in some]
        piece = jnp.concatenate(pieces, axis=0) if len(some) > 1 else pieces[0]
        near = jnp.concatenate([piece] + [swap(piece, mask) for mask in masks], axis=0)
        far = swap(near, 1)
        inputs = [x_own[step] for step in some]
        last = some is rounds[-1]
        grad = accumulate(grad, inputs, near, far, last)
    grad, squares = grad
    grad_squares = dev_parts(squares)

    up = [(i, i + 1) for i in range(groups - 1)]
    down = [(i + 1, i) for i in range(groups - 1)]
    chunks = chunks_of(rows)
    buffers, above, below = [], [], []
    for chunk in chunks:
        piece, *buffers = update(
            layer_owner, weight_squares, grad_squares, grad, master, moment, chunk, buffers
        )
        above.append(piece)
        below.append(piece)
    new_weights, new_master, new_moment = buffers
    for step in range(1, groups):
        for number, chunk in enumerate(chunks):
            above[number] = lax.ppermute(above[number], "grp", up)
            below[number] = lax.ppermute(below[number], "grp", down)
            new_weights = place(layer_owner, new_weights, above[number], below[number], step, chunk)
    return (new_master[None], new_moment[None], new_weights, new_table[None])


def update_table(table, grads, ids, counts):
    devices = lax.axis_size("dev")
    capacity = ids.shape[0] // devices
    slot_rank = jnp.arange(devices * capacity, dtype=jnp.int32) % capacity
    live = slot_rank < jnp.repeat(counts, capacity)
    tagged = jnp.where(live, ids, -1)
    got_ids = lax.all_to_all(tagged, "dev", split_axis=0, concat_axis=0, tiled=True)
    got_grads = lax.all_to_all(grads, "dev", split_axis=0, concat_axis=0, tiled=True)
    return move_table(table, got_ids, got_grads)


def move_table(table, got_ids, got_grads):
    nblocks = table.shape[0]
    width = table.shape[1] * table.shape[2]
    matches = got_ids[None, :] == jnp.arange(nblocks, dtype=jnp.int32)[:, None]
    block_sum = jnp.dot(
        matches.astype(jnp.bfloat16),
        got_grads.reshape(got_ids.shape[0], width),
        preferred_element_type=jnp.float32,
    )
    hits = jnp.sum(matches.astype(jnp.int32), axis=1)
    flat = table.reshape(nblocks, width)
    w_norm = jnp.sqrt(jnp.sum(flat * flat, axis=1) + eps_norm)
    g_norm = jnp.sqrt(jnp.sum(block_sum * block_sum, axis=1) + eps_norm)
    block_trust = w_norm / (g_norm + table_decay * w_norm)
    moved = flat - table_rate * block_trust[:, None] * (block_sum + table_decay * flat)
    return jnp.where((hits > 0)[:, None], moved, flat).reshape(table.shape)


def solution(mesh):
    return jax.shard_map(
        local,
        mesh=mesh,
        in_specs=(
            P(None, "grp", "dev"),
            P(None, ("grp", "dev"), None),
            P(),
            P("grp", "dev", None),
            P("grp", "dev", None),
            P("grp", "dev", None, None),
            P("grp", "dev", None, None, None),
            P("grp", "dev", None),
            P("grp", "dev", None),
        ),
        out_specs=(
            P("grp", "dev", None),
            P("grp", "dev", None),
            P(None, "dev", None),
            P("grp", "dev", None, None),
        ),
        check_vma=False,
    )
```

```python
import jax
import jax.numpy as jnp
from jax import lax
from jax.experimental import pallas as pl
from jax.experimental.pallas import tpu as pltpu
from jax.sharding import PartitionSpec as P


tower_rate = 0.5
momentum_keep = 0.9
tower_decay = 0.1
table_rate = 0.5
table_decay = 0.2
eps_norm = 1e-06
weight_parts = (2, 4, 2)
lanes = 128
mib = 1 << 20


anywhere = pl.BlockSpec(memory_space=pl.ANY)


def layer_of(owner_ref, target):
    return sum(jnp.where(owner_ref[layer] == target, layer, 0) for layer in range(owner_ref.shape[0]))


def chunks_of(rows):
    unit = rows // sum(weight_parts)
    starts = [unit * sum(weight_parts[:i]) for i in range(len(weight_parts))]
    return [(start, unit * part) for start, part in zip(starts, weight_parts)]


def pick(layer_owner, value, steps):
    groups = lax.axis_size("grp")
    count = len(steps)

    def kernel(owner_ref, value_ref, *refs):
        sems = refs[count]
        group = lax.axis_index("grp")
        copies = [
            pltpu.make_async_copy(
                value_ref.at[layer_of(owner_ref, lax.rem(group + step, groups))],
                refs[i],
                sems.at[i],
            )
            for i, step in enumerate(steps)
        ]
        for copy in copies:
            copy.start()
        for copy in copies:
            copy.wait()

    shape = value.shape[1:]
    return pl.pallas_call(
        kernel,
        grid_spec=pltpu.PrefetchScalarGridSpec(
            num_scalar_prefetch=1,
            grid=(1,),
            in_specs=[anywhere],
            out_specs=[pl.BlockSpec(shape, lambda i, owner: (0, 0))] * count,
            scratch_shapes=[pltpu.SemaphoreType.DMA((count,))],
        ),
        out_shape=[jax.ShapeDtypeStruct(shape, value.dtype)] * count,
        compiler_params=pltpu.CompilerParams(vmem_limit_bytes=56 * mib),
        cost_estimate=pl.CostEstimate(
            flops=0, bytes_accessed=4 * count * shape[0] * shape[1], transcendentals=0
        ),
        name="pick",
    )(layer_owner, value)


def pick_transposed(layer_owner, value, step):
    groups = lax.axis_size("grp")
    tokens, rows = value.shape[1:]
    tile = min(tokens, 256)

    def kernel(owner_ref, value_ref, out_ref):
        out_ref[...] = value_ref[0].T

    def source(i, owner_ref):
        target = lax.rem(lax.axis_index("grp") + step, groups)
        return layer_of(owner_ref, target), i, 0

    return pl.pallas_call(
        kernel,
        grid_spec=pltpu.PrefetchScalarGridSpec(
            num_scalar_prefetch=1,
            grid=(tokens // tile,),
            in_specs=[pl.BlockSpec((1, tile, rows), source)],
            out_specs=pl.BlockSpec((rows, tile), lambda i, owner: (0, i)),
        ),
        out_shape=jax.ShapeDtypeStruct((rows, tokens), value.dtype),
        compiler_params=pltpu.CompilerParams(vmem_limit_bytes=56 * mib),
        cost_estimate=pl.CostEstimate(
            flops=0, bytes_accessed=4 * rows * tokens, transcendentals=0
        ),
        name="pick_transposed",
    )(layer_owner, value)


def accumulate(acc, inputs, pieces, last):
    rows, tokens = inputs.shape
    per_dev, columns = pieces[0].shape
    tile = min(columns, 512)
    tiles = columns // tile

    def kernel(*refs):
        refs = list(refs)
        acc_ref = refs.pop(0) if acc is not None else None
        x_ref = refs.pop(0)
        piece_refs, refs = refs[: len(pieces)], refs[len(pieces) :]
        out_ref = refs.pop(0)
        square_ref = refs.pop(0) if last else None
        x_all, g_all, x_sem, g_sem = refs
        column = pl.program_id(0)
        device = lax.axis_index("dev")

        @pl.when(column == 0)
        def _():
            pltpu.make_async_copy(x_ref, x_all, x_sem).start()
            for t in range(tiles):
                for mask, ref in enumerate(piece_refs):
                    first = pl.multiple_of((device ^ mask) * per_dev, per_dev)
                    pltpu.make_async_copy(
                        ref.at[:, pl.ds(t * tile, tile)],
                        g_all.at[t, pl.ds(first, per_dev)],
                        g_sem.at[t],
                    ).start()
            pltpu.make_async_copy(x_all, x_all, x_sem).wait()

        pltpu.make_async_copy(g_all.at[column], g_all.at[column], g_sem.at[column]).wait()
        total = jnp.dot(x_all[...], g_all[column], preferred_element_type=jnp.float32)
        if acc is not None:
            total = total + acc_ref[...]
        out_ref[...] = total
        if last:
            squares = jnp.sum(total * total, axis=0, keepdims=True)
            folded = sum(squares[:, k * lanes : (k + 1) * lanes] for k in range(tile // lanes))

            @pl.when(column == 0)
            def _():
                square_ref[...] = folded

            @pl.when(column > 0)
            def _():
                square_ref[...] += folded

    block = pl.BlockSpec((rows, tile), lambda j: (0, j))
    operands = ([acc] if acc is not None else []) + [inputs, *pieces]
    out_shape = [jax.ShapeDtypeStruct((rows, columns), jnp.float32)]
    out_specs = [block]
    if last:
        out_shape.append(jax.ShapeDtypeStruct((1, lanes), jnp.float32))
        out_specs.append(pl.BlockSpec((1, lanes), lambda j: (0, 0)))
    result = pl.pallas_call(
        kernel,
        grid=(tiles,),
        in_specs=([block] if acc is not None else []) + [anywhere] * (1 + len(pieces)),
        out_specs=out_specs,
        out_shape=out_shape,
        scratch_shapes=[
            pltpu.VMEM((rows, tokens), jnp.bfloat16),
            pltpu.VMEM((tiles, tokens, tile), jnp.bfloat16),
            pltpu.SemaphoreType.DMA,
            pltpu.SemaphoreType.DMA((tiles,)),
        ],
        compiler_params=pltpu.CompilerParams(
            vmem_limit_bytes=2 * tokens * (rows + columns) + 16 * rows * tile + 2 * mib
        ),
        cost_estimate=pl.CostEstimate(
            flops=2 * rows * tokens * columns,
            bytes_accessed=2 * tokens * (rows + columns) + 8 * rows * columns,
            transcendentals=0,
        ),
        name="accumulate",
    )(*operands)
    return result if last else result[0]


def update(layer_owner, weight_squares, grad_squares, grad, master, moment, chunk, buffers):
    groups = lax.axis_size("grp")
    rows, columns = grad.shape
    start, height = chunk
    step = min(32, rows // sum(weight_parts))
    first, steps = start // step, height // step
    count = len(weight_squares)

    def kernel(owner_ref, *refs):
        refs = list(refs)
        weight_refs = [refs.pop(0) for _ in range(count)]
        grad_refs = [refs.pop(0) for _ in range(count)]
        grad_ref, master_ref, moment_ref = refs[:3]
        piece_ref, weights_out, master_out, moment_out = refs[-4:]

        def norm(parts):
            total = sum(ref[...] for ref in parts)
            return jnp.sqrt(jnp.sum(total, axis=1, keepdims=True) + eps_norm)

        weight_norm = norm(weight_refs)
        trust = weight_norm / (norm(grad_refs) + tower_decay * weight_norm)
        value = master_ref[...]
        new_moment = momentum_keep * moment_ref[...] + tower_rate * trust * (
            grad_ref[...] + tower_decay * value
        )
        new_master = value - new_moment
        moment_out[...] = new_moment
        master_out[...] = new_master
        piece = new_master.astype(jnp.bfloat16)
        piece_ref[...] = piece
        weights_out[0] = piece

    vector = pl.BlockSpec((1, lanes), lambda i, owner: (0, 0))
    block = pl.BlockSpec((step, columns), lambda i, owner: (first + i, 0))
    operands = [layer_owner, *weight_squares, *grad_squares, grad, master, moment]
    taken = len(operands)
    return pl.pallas_call(
        kernel,
        grid_spec=pltpu.PrefetchScalarGridSpec(
            num_scalar_prefetch=1,
            grid=(steps,),
            in_specs=[vector] * (2 * count) + [block] * 3 + [anywhere] * len(buffers),
            out_specs=[
                pl.BlockSpec((step, columns), lambda i, owner: (i, 0)),
                pl.BlockSpec(
                    (1, step, columns),
                    lambda i, owner: (layer_of(owner, lax.axis_index("grp")), first + i, 0),
                ),
                block,
                block,
            ],
        ),
        out_shape=[
            jax.ShapeDtypeStruct((height, columns), jnp.bfloat16),
            jax.ShapeDtypeStruct((groups, rows, columns), jnp.bfloat16),
            jax.ShapeDtypeStruct((rows, columns), jnp.float32),
            jax.ShapeDtypeStruct((rows, columns), jnp.float32),
        ],
        input_output_aliases={taken + i: 1 + i for i in range(len(buffers))},
        compiler_params=pltpu.CompilerParams(vmem_limit_bytes=48 * step * columns + 2 * mib),
        cost_estimate=pl.CostEstimate(
            flops=8 * height * columns, bytes_accessed=24 * height * columns, transcendentals=0
        ),
        name="update",
    )(*operands, *buffers)


def exchanges(groups):
    matchings = [
        [(i, i + 1) for i in range(first, groups - 1, 2)] for first in (0, 1)
    ]
    held = [list(range(groups)) for _ in range(2)]
    seen = [{group} for group in range(groups)]
    swaps = []
    for step in range(groups):
        for chain in (step % 2, 1 - step % 2):
            pairs = matchings[(step + chain) % 2]
            pairs = pairs + [(j, i) for i, j in pairs]
            got = [None] * groups
            for i, j in pairs:
                got[j] = held[chain][i]
            held[chain] = got
            new = [
                source if source is not None and source not in seen[group] else None
                for group, source in enumerate(got)
            ]
            if any(source is not None for source in new):
                swaps.append((step, chain, pairs, new))
            for group, source in enumerate(new):
                seen[group].add(group if source is None else source)
    if any(len(groups_seen) < groups for groups_seen in seen):
        raise ValueError("incomplete exchange")
    batches = []
    for number, (*_, new) in enumerate(swaps):
        for batch in batches:
            if all(
                source is None or all(swaps[other][3][group] is None for other in batch)
                for group, source in enumerate(new)
            ):
                batch.append(number)
                break
        else:
            batches.append([number])
    return swaps, sorted(batches, key=lambda batch: batch[-1])


def place(layer_owner, weights, pieces, sources, chunk):
    columns = pieces[0].shape[1]
    start, height = chunk
    count = len(pieces)

    def kernel(owner_ref, weights_ref, *refs):
        piece_refs = refs[:count]
        out_ref, held, in_sem, out_sem = refs[count:]
        group = lax.axis_index("grp")

        def select(values):
            return sum(jnp.where(group == i, value, 0) for i, value in enumerate(values))

        for ref, some in zip(piece_refs, sources):

            @pl.when(select([int(source is not None) for source in some]) > 0)
            def _():
                source = select([0 if source is None else source for source in some])
                inward = pltpu.make_async_copy(ref, held, in_sem)
                inward.start()
                inward.wait()
                layer = layer_of(owner_ref, source)
                outward = pltpu.make_async_copy(
                    held, out_ref.at[layer, pl.ds(start, height)], out_sem
                )
                outward.start()
                outward.wait()

    return pl.pallas_call(
        kernel,
        grid_spec=pltpu.PrefetchScalarGridSpec(
            num_scalar_prefetch=1,
            grid=(1,),
            in_specs=[anywhere] * (1 + count),
            out_specs=anywhere,
            scratch_shapes=[
                pltpu.VMEM((height, columns), jnp.bfloat16),
                pltpu.SemaphoreType.DMA,
                pltpu.SemaphoreType.DMA,
            ],
        ),
        out_shape=jax.ShapeDtypeStruct(weights.shape, weights.dtype),
        input_output_aliases={1: 0},
        compiler_params=pltpu.CompilerParams(vmem_limit_bytes=2 * height * columns + 2 * mib),
        cost_estimate=pl.CostEstimate(
            flops=0, bytes_accessed=4 * height * columns, transcendentals=0
        ),
        name="place",
    )(layer_owner, weights, *pieces)


def shifts_of(groups):
    shifts = [0]
    for step in range(1, groups // 2 + 1):
        shifts += [step] if 2 * step == groups else [step, groups - step]
    return shifts


def local(
    layer_inputs,
    output_grads,
    layer_owner,
    master_weights,
    momentum,
    table_blocks,
    block_grads,
    block_ids,
    block_counts,
):
    groups = lax.axis_size("grp")
    devices = lax.axis_size("dev")
    masks = range(2, devices, 2)

    def swap(value, mask):
        return lax.ppermute(value, "dev", [(i, i ^ mask) for i in range(devices)])

    def shift(value, step):
        if step == 0:
            return value
        return lax.ppermute(value, "grp", [(i, (i + step) % groups) for i in range(groups)])

    def dev_parts(value):
        pair = value + swap(value, 1)
        return [pair] + [swap(pair, mask) for mask in masks]

    master = master_weights[0]
    moment = momentum[0]
    rows, columns = master.shape

    shifts = shifts_of(groups)
    g_own = dict(zip(shifts, pick(layer_owner, output_grads, shifts)))
    x_own = {}
    for step in shifts:
        x_own[step] = pick_transposed(layer_owner, layer_inputs, step)
    g_own = {step: shift(g_own[step], step) for step in shifts}
    x_own = {step: shift(x_own[step], step) for step in shifts}
    new_table = update_table(table_blocks[0], block_grads[0, 0], block_ids[0, 0], block_counts[0, 0])

    squares = jnp.sum(master * master, axis=0, keepdims=True)
    squares = jnp.sum(squares.reshape(columns // lanes, lanes), axis=0, keepdims=True)
    weight_squares = dev_parts(squares)

    grad = None
    for step in shifts:
        pieces = [None] * devices
        for mask in range(0, devices, 2):
            pieces[mask] = swap(g_own[step], mask) if mask else g_own[step]
            pieces[mask + 1] = swap(pieces[mask], 1)
        grad = accumulate(grad, x_own[step], pieces, step == shifts[-1])
    grad, squares = grad
    grad_squares = dev_parts(squares)

    chunks = chunks_of(rows)
    swaps, batches = exchanges(groups)
    buffers, held = [], []
    for chunk in chunks:
        piece, *buffers = update(
            layer_owner, weight_squares, grad_squares, grad, master, moment, chunk, buffers
        )
        held.append([piece, piece])
    new_weights, new_master, new_moment = buffers
    pieces = {}
    for number, (_, chain, pairs, _) in enumerate(swaps):
        for chunk in range(len(chunks)):
            piece = lax.ppermute(held[chunk][chain], "grp", pairs)
            pieces[number, chunk] = held[chunk][chain] = piece
    for batch in batches:
        for number, chunk in enumerate(chunks):
            new_weights = place(
                layer_owner,
                new_weights,
                [pieces[step, number] for step in batch],
                [swaps[step][3] for step in batch],
                chunk,
            )
    return (new_master[None], new_moment[None], new_weights, new_table[None])


def update_table(table, grads, ids, counts):
    devices = lax.axis_size("dev")
    capacity = ids.shape[0] // devices
    slot_rank = jnp.arange(devices * capacity, dtype=jnp.int32) % capacity
    live = slot_rank < jnp.repeat(counts, capacity)
    tagged = jnp.where(live, ids, -1)
    got_ids = lax.all_to_all(tagged, "dev", split_axis=0, concat_axis=0, tiled=True)
    got_grads = lax.all_to_all(grads, "dev", split_axis=0, concat_axis=0, tiled=True)
    return move_table(table, got_ids, got_grads)


def move_table(table, got_ids, got_grads):
    nblocks = table.shape[0]
    width = table.shape[1] * table.shape[2]
    matches = got_ids[None, :] == jnp.arange(nblocks, dtype=jnp.int32)[:, None]
    block_sum = jnp.dot(
        matches.astype(jnp.bfloat16),
        got_grads.reshape(got_ids.shape[0], width),
        preferred_element_type=jnp.float32,
    )
    hits = jnp.sum(matches.astype(jnp.int32), axis=1)
    flat = table.reshape(nblocks, width)
    w_norm = jnp.sqrt(jnp.sum(flat * flat, axis=1) + eps_norm)
    g_norm = jnp.sqrt(jnp.sum(block_sum * block_sum, axis=1) + eps_norm)
    block_trust = w_norm / (g_norm + table_decay * w_norm)
    moved = flat - table_rate * block_trust[:, None] * (block_sum + table_decay * flat)
    return jnp.where((hits > 0)[:, None], moved, flat).reshape(table.shape)


def solution(mesh):
    return jax.shard_map(
        local,
        mesh=mesh,
        in_specs=(
            P(None, "grp", "dev"),
            P(None, ("grp", "dev"), None),
            P(),
            P("grp", "dev", None),
            P("grp", "dev", None),
            P("grp", "dev", None, None),
            P("grp", "dev", None, None, None),
            P("grp", "dev", None),
            P("grp", "dev", None),
        ),
        out_specs=(
            P("grp", "dev", None),
            P("grp", "dev", None),
            P(None, "dev", None),
            P("grp", "dev", None, None),
        ),
        check_vma=False,
    )
```

```python
import jax
import jax.numpy as jnp
from jax import lax
from jax.experimental import pallas as pl
from jax.experimental.pallas import tpu as pltpu
from jax.sharding import PartitionSpec as P


tower_rate = 0.5
momentum_keep = 0.9
tower_decay = 0.1
table_rate = 0.5
table_decay = 0.2
eps_norm = 1e-06
weight_parts = (1, 2, 4, 1)
lanes = 128
mib = 1 << 20


anywhere = pl.BlockSpec(memory_space=pl.ANY)


def layer_of(owner_ref, target):
    return sum(jnp.where(owner_ref[layer] == target, layer, 0) for layer in range(owner_ref.shape[0]))


def chunks_of(rows):
    unit = rows // sum(weight_parts)
    starts = [unit * sum(weight_parts[:i]) for i in range(len(weight_parts))]
    return [(start, unit * part) for start, part in zip(starts, weight_parts)]


def pick(layer_owner, value, steps):
    groups = lax.axis_size("grp")
    count = len(steps)

    def kernel(owner_ref, value_ref, *refs):
        sems = refs[count]
        group = lax.axis_index("grp")
        copies = [
            pltpu.make_async_copy(
                value_ref.at[layer_of(owner_ref, lax.rem(group + step, groups))],
                refs[i],
                sems.at[i],
            )
            for i, step in enumerate(steps)
        ]
        for copy in copies:
            copy.start()
        for copy in copies:
            copy.wait()

    shape = value.shape[1:]
    return pl.pallas_call(
        kernel,
        grid_spec=pltpu.PrefetchScalarGridSpec(
            num_scalar_prefetch=1,
            grid=(1,),
            in_specs=[anywhere],
            out_specs=[pl.BlockSpec(shape, lambda i, owner: (0, 0))] * count,
            scratch_shapes=[pltpu.SemaphoreType.DMA((count,))],
        ),
        out_shape=[jax.ShapeDtypeStruct(shape, value.dtype)] * count,
        compiler_params=pltpu.CompilerParams(vmem_limit_bytes=56 * mib),
        cost_estimate=pl.CostEstimate(
            flops=0, bytes_accessed=4 * count * shape[0] * shape[1], transcendentals=0
        ),
        name="pick",
    )(layer_owner, value)


def pick_transposed(layer_owner, value, step, start, count):
    groups = lax.axis_size("grp")
    rows = value.shape[2]
    tile = min(count, 256)
    first = start // tile

    def kernel(owner_ref, value_ref, out_ref):
        out_ref[...] = value_ref[0].T

    def source(i, owner_ref):
        target = lax.rem(lax.axis_index("grp") + step, groups)
        return layer_of(owner_ref, target), first + i, 0

    return pl.pallas_call(
        kernel,
        grid_spec=pltpu.PrefetchScalarGridSpec(
            num_scalar_prefetch=1,
            grid=(count // tile,),
            in_specs=[pl.BlockSpec((1, tile, rows), source)],
            out_specs=pl.BlockSpec((rows, tile), lambda i, owner: (0, i)),
        ),
        out_shape=jax.ShapeDtypeStruct((rows, count), value.dtype),
        compiler_params=pltpu.CompilerParams(vmem_limit_bytes=56 * mib),
        cost_estimate=pl.CostEstimate(
            flops=0, bytes_accessed=4 * rows * count, transcendentals=0
        ),
        name="pick_transposed",
    )(layer_owner, value)


def accumulate(acc, inputs, pieces):
    rows, tokens = inputs.shape
    per_dev, columns = pieces[0].shape
    tile = min(columns, 512)
    tiles = columns // tile

    def kernel(*refs):
        refs = list(refs)
        acc_ref = refs.pop(0) if acc is not None else None
        x_ref = refs.pop(0)
        piece_refs, refs = refs[: len(pieces)], refs[len(pieces) :]
        out_ref = refs.pop(0)
        x_all, g_all, x_sem, g_sem = refs
        column = pl.program_id(0)
        device = lax.axis_index("dev")

        @pl.when(column == 0)
        def _():
            pltpu.make_async_copy(x_ref, x_all, x_sem).start()
            for t in range(tiles):
                for mask, ref in enumerate(piece_refs):
                    first = pl.multiple_of((device ^ mask) * per_dev, per_dev)
                    pltpu.make_async_copy(
                        ref.at[:, pl.ds(t * tile, tile)],
                        g_all.at[t, pl.ds(first, per_dev)],
                        g_sem.at[t],
                    ).start()
            pltpu.make_async_copy(x_all, x_all, x_sem).wait()

        pltpu.make_async_copy(g_all.at[column], g_all.at[column], g_sem.at[column]).wait()
        total = jnp.dot(x_all[...], g_all[column], preferred_element_type=jnp.float32)
        if acc is not None:
            total = total + acc_ref[...]
        out_ref[...] = total

    block = pl.BlockSpec((rows, tile), lambda j: (0, j))
    operands = ([acc] if acc is not None else []) + [inputs, *pieces]
    return pl.pallas_call(
        kernel,
        grid=(tiles,),
        in_specs=([block] if acc is not None else []) + [anywhere] * (1 + len(pieces)),
        out_specs=block,
        out_shape=jax.ShapeDtypeStruct((rows, columns), jnp.float32),
        scratch_shapes=[
            pltpu.VMEM((rows, tokens), jnp.bfloat16),
            pltpu.VMEM((tiles, tokens, tile), jnp.bfloat16),
            pltpu.SemaphoreType.DMA,
            pltpu.SemaphoreType.DMA((tiles,)),
        ],
        compiler_params=pltpu.CompilerParams(
            vmem_limit_bytes=2 * tokens * (rows + columns) + 16 * rows * tile + 2 * mib
        ),
        cost_estimate=pl.CostEstimate(
            flops=2 * rows * tokens * columns,
            bytes_accessed=2 * tokens * (rows + columns) + 8 * rows * columns,
            transcendentals=0,
        ),
        name="accumulate",
    )(*operands)


def arrange(pieces):
    per_dev, columns = pieces[0].shape
    devices = len(pieces)

    def kernel(*refs):
        piece_refs, (out_ref, sem) = refs[:devices], refs[devices:]
        device = lax.axis_index("dev")
        for mask, ref in enumerate(piece_refs):
            first = pl.multiple_of((device ^ mask) * per_dev, per_dev)
            pltpu.make_async_copy(ref, out_ref.at[pl.ds(first, per_dev)], sem).start()
        pltpu.make_async_copy(out_ref, out_ref, sem).wait()

    return pl.pallas_call(
        kernel,
        in_specs=[anywhere] * devices,
        out_specs=pl.BlockSpec(memory_space=pltpu.VMEM),
        out_shape=jax.ShapeDtypeStruct((devices * per_dev, columns), pieces[0].dtype),
        scratch_shapes=[pltpu.SemaphoreType.DMA],
        compiler_params=pltpu.CompilerParams(
            vmem_limit_bytes=4 * devices * per_dev * columns + 2 * mib
        ),
        cost_estimate=pl.CostEstimate(
            flops=0, bytes_accessed=4 * devices * per_dev * columns, transcendentals=0
        ),
        name="arrange",
    )(*pieces)


def update(layer_owner, weight_squares, grad_squares, grad, master, moment, chunk, buffers):
    groups = lax.axis_size("grp")
    rows, columns = grad.shape
    start, height = chunk
    step = min(32, rows // sum(weight_parts))
    first, steps = start // step, height // step
    count = len(weight_squares)

    def kernel(owner_ref, *refs):
        refs = list(refs)
        weight_refs = [refs.pop(0) for _ in range(count)]
        grad_refs = [refs.pop(0) for _ in range(count)]
        grad_ref, master_ref, moment_ref = refs[:3]
        piece_ref, weights_out, master_out, moment_out = refs[-4:]

        def norm(parts):
            total = sum(ref[...] for ref in parts)
            return jnp.sqrt(jnp.sum(total, axis=1, keepdims=True) + eps_norm)

        weight_norm = norm(weight_refs)
        trust = weight_norm / (norm(grad_refs) + tower_decay * weight_norm)
        value = master_ref[...]
        new_moment = momentum_keep * moment_ref[...] + tower_rate * trust * (
            grad_ref[...] + tower_decay * value
        )
        new_master = value - new_moment
        moment_out[...] = new_moment
        master_out[...] = new_master
        piece = new_master.astype(jnp.bfloat16)
        piece_ref[...] = piece
        weights_out[0] = piece

    vector = pl.BlockSpec((1, lanes), lambda i, owner: (0, 0))
    block = pl.BlockSpec((step, columns), lambda i, owner: (first + i, 0))
    operands = [layer_owner, *weight_squares, *grad_squares, grad, master, moment]
    taken = len(operands)
    return pl.pallas_call(
        kernel,
        grid_spec=pltpu.PrefetchScalarGridSpec(
            num_scalar_prefetch=1,
            grid=(steps,),
            in_specs=[vector] * (2 * count) + [block] * 3 + [anywhere] * len(buffers),
            out_specs=[
                pl.BlockSpec((step, columns), lambda i, owner: (i, 0)),
                pl.BlockSpec(
                    (1, step, columns),
                    lambda i, owner: (layer_of(owner, lax.axis_index("grp")), first + i, 0),
                ),
                block,
                block,
            ],
        ),
        out_shape=[
            jax.ShapeDtypeStruct((height, columns), jnp.bfloat16),
            jax.ShapeDtypeStruct((groups, rows, columns), jnp.bfloat16),
            jax.ShapeDtypeStruct((rows, columns), jnp.float32),
            jax.ShapeDtypeStruct((rows, columns), jnp.float32),
        ],
        input_output_aliases={taken + i: 1 + i for i in range(len(buffers))},
        compiler_params=pltpu.CompilerParams(vmem_limit_bytes=48 * step * columns + 2 * mib),
        cost_estimate=pl.CostEstimate(
            flops=8 * height * columns, bytes_accessed=24 * height * columns, transcendentals=0
        ),
        name="update",
    )(*operands, *buffers)


def exchanges(groups):
    matchings = [
        [(i, i + 1) for i in range(first, groups - 1, 2)] for first in (0, 1)
    ]
    held = [list(range(groups)) for _ in range(2)]
    seen = [{group} for group in range(groups)]
    swaps = []
    for step in range(groups):
        for chain in (step % 2, 1 - step % 2):
            pairs = matchings[(step + chain) % 2]
            pairs = pairs + [(j, i) for i, j in pairs]
            got = [None] * groups
            for i, j in pairs:
                got[j] = held[chain][i]
            held[chain] = got
            new = [
                source if source is not None and source not in seen[group] else None
                for group, source in enumerate(got)
            ]
            if any(source is not None for source in new):
                swaps.append((step, chain, pairs, new))
            for group, source in enumerate(new):
                seen[group].add(group if source is None else source)
    if any(len(groups_seen) < groups for groups_seen in seen):
        raise ValueError("incomplete exchange")
    batches = []
    for number, (*_, new) in enumerate(swaps):
        for batch in batches:
            if all(
                source is None or all(swaps[other][3][group] is None for other in batch)
                for group, source in enumerate(new)
            ):
                batch.append(number)
                break
        else:
            batches.append([number])
    return swaps, sorted(batches, key=lambda batch: batch[-1])


def place(layer_owner, weights, pieces, sources, chunk):
    columns = pieces[0].shape[1]
    start, height = chunk
    count = len(pieces)

    def kernel(owner_ref, weights_ref, *refs):
        piece_refs = refs[:count]
        out_ref, held, in_sem, out_sem = refs[count:]
        group = lax.axis_index("grp")

        def select(values):
            return sum(jnp.where(group == i, value, 0) for i, value in enumerate(values))

        for ref, some in zip(piece_refs, sources):

            @pl.when(select([int(source is not None) for source in some]) > 0)
            def _():
                source = select([0 if source is None else source for source in some])
                inward = pltpu.make_async_copy(ref, held, in_sem)
                inward.start()
                inward.wait()
                layer = layer_of(owner_ref, source)
                outward = pltpu.make_async_copy(
                    held, out_ref.at[layer, pl.ds(start, height)], out_sem
                )
                outward.start()
                outward.wait()

    return pl.pallas_call(
        kernel,
        grid_spec=pltpu.PrefetchScalarGridSpec(
            num_scalar_prefetch=1,
            grid=(1,),
            in_specs=[anywhere] * (1 + count),
            out_specs=anywhere,
            scratch_shapes=[
                pltpu.VMEM((height, columns), jnp.bfloat16),
                pltpu.SemaphoreType.DMA,
                pltpu.SemaphoreType.DMA,
            ],
        ),
        out_shape=jax.ShapeDtypeStruct(weights.shape, weights.dtype),
        input_output_aliases={1: 0},
        compiler_params=pltpu.CompilerParams(vmem_limit_bytes=2 * height * columns + 2 * mib),
        cost_estimate=pl.CostEstimate(
            flops=0, bytes_accessed=4 * height * columns, transcendentals=0
        ),
        name="place",
    )(layer_owner, weights, *pieces)


def shifts_of(groups):
    shifts = [0]
    for step in range(1, groups // 2 + 1):
        shifts += [step] if 2 * step == groups else [step, groups - step]
    return shifts


def local(
    layer_inputs,
    output_grads,
    layer_owner,
    master_weights,
    momentum,
    table_blocks,
    block_grads,
    block_ids,
    block_counts,
):
    groups = lax.axis_size("grp")
    devices = lax.axis_size("dev")
    masks = range(devices - 2, 0, -2)

    def swap(value, mask):
        return lax.ppermute(value, "dev", [(i, i ^ mask) for i in range(devices)])

    def shift(value, step):
        if step == 0:
            return value
        return lax.ppermute(value, "grp", [(i, (i + step) % groups) for i in range(groups)])

    def fold(value):
        squares = jnp.sum(value * value, axis=0, keepdims=True)
        return jnp.sum(squares.reshape(-1, lanes), axis=0, keepdims=True)

    def dev_parts(value):
        pair = value + swap(value, 1)
        return [pair] + [swap(pair, mask) for mask in masks]

    master = master_weights[0]
    moment = momentum[0]
    rows, _ = master.shape

    shifts = shifts_of(groups)
    g_own = dict(zip(shifts[1:2], pick(layer_owner, output_grads, shifts[1:2])))
    rest = shifts[:1] + shifts[2:]
    g_own.update(zip(rest, pick(layer_owner, output_grads, rest)))
    g_own = {step: shift(g_own[step], step) for step in shifts}
    tokens = layer_inputs.shape[1]
    early = tokens * 3 // 4

    def inputs_of(step, start, count):
        value = pick_transposed(layer_owner, layer_inputs, step, start, count)
        return shift(value, step)

    x_own = {step: inputs_of(step, 0, tokens) for step in shifts[:-1]}
    x_early = inputs_of(shifts[-1], 0, early)
    x_late = inputs_of(shifts[-1], early, tokens - early)
    new_table = update_table(table_blocks[0], block_grads[0, 0], block_ids[0, 0], block_counts[0, 0])

    weight_squares = dev_parts(fold(master))

    grad = None
    for step in shifts:
        pieces = [None] * devices
        for mask in range(0, devices, 2):
            pieces[mask] = swap(g_own[step], mask) if mask else g_own[step]
            pieces[mask + 1] = swap(pieces[mask], 1)
        if step != shifts[-1]:
            grad = accumulate(grad, x_own[step], pieces)
    cotangents = arrange(pieces)
    grad = grad + jnp.dot(x_early, cotangents[:early], preferred_element_type=jnp.float32)
    grad = lax.optimization_barrier(grad)
    grad = grad + jnp.dot(x_late, cotangents[early:], preferred_element_type=jnp.float32)
    squares = fold(grad)
    grad_squares = dev_parts(squares)

    chunks = chunks_of(rows)
    swaps, batches = exchanges(groups)
    buffers, held = [], []
    for chunk in chunks:
        piece, *buffers = update(
            layer_owner, weight_squares, grad_squares, grad, master, moment, chunk, buffers
        )
        held.append([piece, piece])
    new_weights, new_master, new_moment = buffers
    pieces = {}
    for number, (_, chain, pairs, _) in enumerate(swaps):
        for chunk in range(len(chunks)):
            piece = lax.ppermute(held[chunk][chain], "grp", pairs)
            pieces[number, chunk] = held[chunk][chain] = piece
    for batch in batches:
        for number, chunk in enumerate(chunks):
            new_weights = place(
                layer_owner,
                new_weights,
                [pieces[step, number] for step in batch],
                [swaps[step][3] for step in batch],
                chunk,
            )
    return (new_master[None], new_moment[None], new_weights, new_table[None])


def update_table(table, grads, ids, counts):
    devices = lax.axis_size("dev")
    capacity = ids.shape[0] // devices
    slot_rank = jnp.arange(devices * capacity, dtype=jnp.int32) % capacity
    live = slot_rank < jnp.repeat(counts, capacity)
    tagged = jnp.where(live, ids, -1)
    got_ids = lax.all_to_all(tagged, "dev", split_axis=0, concat_axis=0, tiled=True)
    got_grads = lax.all_to_all(grads, "dev", split_axis=0, concat_axis=0, tiled=True)
    return move_table(table, got_ids, got_grads)


def move_table(table, got_ids, got_grads):
    nblocks = table.shape[0]
    width = table.shape[1] * table.shape[2]
    matches = got_ids[None, :] == jnp.arange(nblocks, dtype=jnp.int32)[:, None]
    block_sum = jnp.dot(
        matches.astype(jnp.bfloat16),
        got_grads.reshape(got_ids.shape[0], width),
        preferred_element_type=jnp.float32,
    )
    hits = jnp.sum(matches.astype(jnp.int32), axis=1)
    flat = table.reshape(nblocks, width)
    w_norm = jnp.sqrt(jnp.sum(flat * flat, axis=1) + eps_norm)
    g_norm = jnp.sqrt(jnp.sum(block_sum * block_sum, axis=1) + eps_norm)
    block_trust = w_norm / (g_norm + table_decay * w_norm)
    moved = flat - table_rate * block_trust[:, None] * (block_sum + table_decay * flat)
    return jnp.where((hits > 0)[:, None], moved, flat).reshape(table.shape)


def solution(mesh):
    return jax.shard_map(
        local,
        mesh=mesh,
        in_specs=(
            P(None, "grp", "dev"),
            P(None, ("grp", "dev"), None),
            P(),
            P("grp", "dev", None),
            P("grp", "dev", None),
            P("grp", "dev", None, None),
            P("grp", "dev", None, None, None),
            P("grp", "dev", None),
            P("grp", "dev", None),
        ),
        out_specs=(
            P("grp", "dev", None),
            P("grp", "dev", None),
            P(None, "dev", None),
            P("grp", "dev", None, None),
        ),
        check_vma=False,
    )
```
